32 devices in a mesh: tile: 2 (over y), wave: 16 (over z, x, core).
Axes of the slice: x: 2, y: 2, z: 4, core: 2. Of those that a mesh axis runs over, the one named last changes fastest.
Arguments:
- frames: float32 [4, 1024, 4096], P(None, ('tile', 'wave')), parts along dimension 1, may hold values from -6 to 6
- inverse_var: float32 [4, 1024, 4096], P(None, ('tile', 'wave')), parts along dimension 1, may hold values from 0.2 to 240
- masked: int32 [4, 1024, 4096], P(None, ('tile', 'wave')), parts along dimension 1, may hold values 0 or 1
- psf_band: float32 [4, 1024, 16], P(None, ('tile', 'wave')), parts along dimension 1, may hold values from 0.02 to 0.2
- offsets: int32 [32], P(('tile', 'wave')), parts along dimension 0, may hold values from 18 to 31
- starts: int32 [32, 500], P(('tile', 'wave')), parts along dimension 0, may hold values from 0 to 3995, as said below
- profile: float32 [32, 12, 500], P(('tile', 'wave')), parts along dimension 0, may hold values from 0.05 to 0.5
- flux_start: float32 [1024, 500], P(('tile', 'wave')), parts along dimension 0, may hold values from -3 to 3
Outputs:
- solution: float32 [1024, 500], P(('tile', 'wave')), parts along dimension 0
- residual: float32 [1024, 500], P(('tile', 'wave')), parts along dimension 0
The draws below stay inside these ranges and needn't reach their ends.
There are 2 independent parts, one for each index of `tile`. The reference program is written for one: setup_inputs(seed, part) draws one part's arguments, and reference() takes and returns one part's arrays. A program takes and returns all parts, laid end to end along the dimension named above; each array names one. Nothing has to cross between parts.
Inputs may be any that keep to these rules, and one draw needn't show every extreme that they name: In every slab, fiber k's trace starts at a column from 8k to 8k + 3, so the fibers lie in order, 8 columns apart give or take 3, and neighbouring profiles intersect.
All inputs are finite; a program needn't handle non-finite values. No bound on the sum of `masked` on one device may be relied on, other than what follows from the above.
Results may differ from the reference program's by a relative error of at most 0.0003.
Values sent between devices are 32-bit elements; how exact they have to be, the bound alone decides.
A program may use at most 64 MiB of HBM per device.

```python
import math
import jax
import jax.numpy as jnp
from jax import lax

FIB = 500
COLS = 4096
EXPO = 4
SLAB_ROWS = 32
ITERS = 3
HALO = 32
BAND = 16
PW = 12
SLABS = 16
WAVES = 512


def draw_inverse_var(key, part):
    first_key, second_key = jax.random.split(jax.random.fold_in(key, 11), 2)
    row_index = jnp.arange(WAVES, dtype=jnp.float32)
    ramp = 3.0 ** (row_index / WAVES)
    row_scale = 10.0 ** jax.random.uniform(second_key, (1, WAVES, 1), jnp.float32, 0.0, 1.0)
    pixels = jnp.exp(jax.random.uniform(first_key, (EXPO, WAVES, COLS), jnp.float32, math.log(0.3), math.log(3.0)))
    return pixels * row_scale * ramp[None, :, None]


def draw_starts(key, part):
    pitch = (COLS - PW - 4) // FIB
    jitter = jax.random.randint(jax.random.fold_in(key, 23), (SLABS, FIB), 0, 4, dtype=jnp.int32)
    return jnp.arange(FIB, dtype=jnp.int32)[None, :] * pitch + jitter


def plant(array, own_key, low, high):
    place = [jax.random.randint(jax.random.fold_in(own_key, axis), (), 0, length) for axis, length in enumerate(array.shape)]
    widest = array.shape.index(max(array.shape))
    beside = place[:widest] + [(place[widest] + 1) % array.shape[widest]] + place[widest + 1:]
    return array.at[tuple(place)].set(low).at[tuple(beside)].set(high)


def block_levels(own_key, shape, cuts, least, high):
    level = 1.0
    for dim, parts in cuts:
        heights = jax.random.uniform(jax.random.fold_in(jax.random.fold_in(own_key, 6), dim), (parts,), jnp.float32, least / len(cuts), high / len(cuts))
        level = level * jnp.repeat(jnp.exp(heights), shape[dim] // parts).reshape((-1,) + (1,) * (len(shape) - 1 - dim))
    return level


def normal_values(key, shape, deviation, bound, shards=(), kind=jnp.bfloat16):
    array = jax.random.normal(key, shape, jnp.float32) * deviation
    if len(shards) > 0:
        array = block_levels(key, shape, shards, -0.22, 0.18) * array
    return jnp.clip(array, min=-bound, max=bound).astype(kind)


def setup_inputs(seed: int = 0, part: int = 0) -> dict:
    streams_of = jax.random.split(jax.random.key(seed), 9)
    own_keys = jax.random.split(jax.random.fold_in(streams_of[8], part), 9)
    return {
        "frames": normal_values(own_keys[0], (EXPO, WAVES, COLS), 1.0, 6.0, ((1, 16),), jnp.float32),
        "inverse_var": draw_inverse_var(jax.random.fold_in(jax.random.fold_in(streams_of[8], part), 71), part),
        "masked": plant((jax.random.randint(own_keys[2], (EXPO, WAVES, COLS), 0, 16) < 1).astype(jnp.int32), jax.random.fold_in(own_keys[2], 1), 0, 1),
        "psf_band": jnp.clip(jnp.exp(math.log(0.2) - 2.3025851 * jax.random.uniform(own_keys[3], (EXPO, WAVES, BAND), jnp.float32) ** block_levels(own_keys[3], (EXPO, WAVES, BAND), ((1, 16),), -0.2, 0.2)), 0.02, 0.2),
        "offsets": plant(jax.random.randint(own_keys[4], (SLABS,), HALO - BAND + 2, HALO), jax.random.fold_in(own_keys[4], 1), HALO - BAND + 2, HALO - 1).astype(jnp.int32),
        "starts": draw_starts(jax.random.fold_in(jax.random.fold_in(streams_of[8], part), 71), part),
        "profile": jnp.clip(jnp.exp(math.log(0.5) - 2.3025851 * jax.random.uniform(own_keys[6], (SLABS, PW, FIB), jnp.float32) ** block_levels(own_keys[6], (SLABS, PW, FIB), ((0, 16),), -0.2, 0.2)), 0.05, 0.5),
        "flux_start": normal_values(own_keys[7], (WAVES, FIB), 0.5, 3.0, ((0, 16),), jnp.float32),
    }


RIDGE = 0.2
PRECISE = lax.Precision.HIGHEST


def row_matrix(band_slab, offset):
    width = SLAB_ROWS + 2 * HALO
    column_index = jnp.arange(width, dtype=jnp.int32)
    row_index = jnp.arange(SLAB_ROWS, dtype=jnp.int32)
    summed = jnp.zeros((band_slab.shape[0], SLAB_ROWS, width), jnp.float32)
    for band_step in range(BAND):
        selector = (column_index[None, :] == row_index[:, None] + offset + band_step).astype(jnp.float32)
        summed = summed + band_slab[:, :, band_step][:, :, None] * selector[None, :, :]
    return summed


def column_profile(starts_row, profile_slab):
    column_index = jnp.arange(COLS, dtype=jnp.int32)[:, None]
    summed = jnp.zeros((COLS, FIB), jnp.float32)
    for column_shift in range(PW):
        selector = (column_index == starts_row[None, :] + column_shift).astype(jnp.float32)
        summed = summed + profile_slab[column_shift][None, :] * selector
    return summed


def project(extended, target, weight, rowmat, colmat):
    interior = jnp.einsum('erx,xk->erk', rowmat, extended, precision=PRECISE)
    predicted = jnp.einsum('erk,ck->erc', interior, colmat, precision=PRECISE)
    weighted = weight * (target - predicted)
    folded_back = jnp.einsum('erc,ck->erk', weighted, colmat, precision=PRECISE)
    return jnp.einsum('erx,erk->xk', rowmat, folded_back, precision=PRECISE)


def diagonal_terms(weight, rowmat, colmat):
    folded_back = jnp.einsum('erc,ck->erk', weight, colmat * colmat, precision=PRECISE)
    return jnp.einsum('erx,erk->xk', rowmat * rowmat, folded_back, precision=PRECISE)


def fold_slabs(pieces):
    width = SLAB_ROWS + 2 * HALO
    positions = (jnp.arange(SLABS, dtype=jnp.int32)[:, None] * SLAB_ROWS + jnp.arange(width, dtype=jnp.int32)[None, :]).reshape(-1)
    summed = jnp.zeros((WAVES + 2 * HALO, FIB), jnp.float32).at[positions].add(pieces.reshape(-1, FIB))
    return summed[HALO:HALO + WAVES]


def reference(frames, inverse_var, masked, psf_band, offsets, starts, profile, flux_start):
    slab_list = jnp.arange(SLABS, dtype=jnp.int32)

    def slab_inputs(slab_index):
        first_row = (slab_index * SLAB_ROWS).astype(jnp.int32)
        rowmat = row_matrix(lax.dynamic_slice_in_dim(psf_band, first_row, SLAB_ROWS, 1), offsets[slab_index])
        colmat = column_profile(starts[slab_index], profile[slab_index])
        flags = lax.dynamic_slice_in_dim(masked, first_row, SLAB_ROWS, 1).astype(jnp.float32)
        weight = lax.dynamic_slice_in_dim(inverse_var, first_row, SLAB_ROWS, 1) * (1.0 - flags)
        return first_row, rowmat, colmat, weight

    def apply_all(values, with_data):
        padded = jnp.pad(values, ((HALO, HALO), (0, 0)))

        def per_slab(slab_index):
            first_row, rowmat, colmat, weight = slab_inputs(slab_index)
            extended = lax.dynamic_slice_in_dim(padded, first_row, SLAB_ROWS + 2 * HALO, 0)
            if with_data:
                target = lax.dynamic_slice_in_dim(frames, first_row, SLAB_ROWS, 1)
            else:
                target = jnp.zeros((), jnp.float32)
            return project(extended, target, weight, rowmat, colmat)

        return fold_slabs(lax.map(per_slab, slab_list))

    def diag_slab(slab_index):
        first_row, rowmat, colmat, weight = slab_inputs(slab_index)
        return diagonal_terms(weight, rowmat, colmat)

    diagonal = fold_slabs(lax.map(diag_slab, slab_list)) + RIDGE
    residual = apply_all(flux_start, True) - RIDGE * flux_start
    solution = flux_start
    scaled = residual / diagonal
    direction = scaled
    energy = jnp.sum(residual * scaled)
    for iteration in range(ITERS):
        image_dir = RIDGE * direction - apply_all(direction, False)
        step_size = energy / jnp.sum(direction * image_dir)
        solution = solution + step_size * direction
        residual = residual - step_size * image_dir
        scaled = residual / diagonal
        energy_new = jnp.sum(residual * scaled)
        direction = scaled + (energy_new / energy) * direction
        energy = energy_new
    return solution, residual
```

```python
import functools

import jax
import jax.numpy as jnp
from jax import lax
from jax.experimental import pallas as pl
from jax.experimental.pallas import tpu as pltpu
from jax.sharding import PartitionSpec as P

RIDGE = 0.2
REACH = 16
PITCH = 8
LANES = 128
SHIFTS = (6.0, 2.0)
F32, BF16 = jnp.float32, jnp.bfloat16
HIGH = lax.Precision.HIGHEST


def split(value):
    hi = value.astype(BF16)
    return hi, (value - hi.astype(F32)).astype(BF16)


def dot(a, b):
    return jnp.dot(a, b, preferred_element_type=F32)


def dot3(a, b):
    return dot(a[0], b[0]) + (dot(a[1], b[0]) + dot(a[0], b[1]))


def dot6(a, b):
    return jnp.dot(a, b, precision=HIGH, preferred_element_type=F32)


def total(value):
    return jnp.sum(value, keepdims=True)


def tri(d, o, y):
    wide = y.shape[1]
    return d * y + o * pltpu.roll(y, 1, 1) + pltpu.roll(o * y, wide - 1, 1)


def kernel(n, fr_hbm, iv_hbm, mk_hbm, band_ref, off_ref, st_ref, pr_ref, fl_ref, x_ref, r_ref,
           fr, iv, mk, pf, st, pk, g, fx, fbu, fbd, pku, pkd, fo, fiu, fid, vx, ra, da, oa, gown, gall,
           load, su, sd, ru, rd, gs, gr, *, chunks):
    expo, rows, cols = fr.shape
    fib = fl_ref.shape[1]
    wide = fx.shape[1]
    er = expo * rows
    span = cols // chunks
    me = lax.axis_index("wave")

    def loads(j):
        part = pl.ds(j * span, span)
        return [
            pltpu.make_async_copy(h.at[:, :, part], v.at[:, :, part], load.at[i, j])
            for i, (h, v) in enumerate(((iv_hbm, iv), (mk_hbm, mk), (fr_hbm, fr)))
        ]

    for j in range(chunks):
        for copy in loads(j):
            copy.start()

    fx[...] = jnp.zeros_like(fx)
    fbu[...] = jnp.zeros_like(fbu)
    fbd[...] = jnp.zeros_like(fbd)
    pku[...] = jnp.zeros_like(pku)
    pkd[...] = jnp.zeros_like(pkd)
    fiu[...] = jnp.zeros_like(fiu)
    fid[...] = jnp.zeros_like(fid)
    vx[...] = jnp.zeros_like(vx)

    barrier = pltpu.get_barrier_semaphore()

    @pl.loop(1, n)
    def _(d):
        pl.semaphore_signal(barrier, inc=1, device_id={"wave": lax.rem(me + d, n)},
                            device_id_type=pl.DeviceIdType.MESH)

    def pair(k, down_src, down_dst, up_src, up_dst):
        down = pltpu.make_async_remote_copy(
            src_ref=down_src, dst_ref=down_dst, send_sem=sd.at[k], recv_sem=rd.at[k],
            device_id={"wave": lax.rem(me + 1, n)}, device_id_type=pl.DeviceIdType.MESH)
        up = pltpu.make_async_remote_copy(
            src_ref=up_src, dst_ref=up_dst, send_sem=su.at[k], recv_sem=ru.at[k],
            device_id={"wave": lax.rem(me + n - 1, n)}, device_id_type=pl.DeviceIdType.MESH)
        return down, up

    def start(copies):
        @pl.when(me < n - 1)
        def _():
            copies[0].start()

        @pl.when(me > 0)
        def _():
            copies[1].start()

    def arrive(copies):
        @pl.when(me > 0)
        def _():
            copies[0].wait_recv()

        @pl.when(me < n - 1)
        def _():
            copies[1].wait_recv()

    def sent(copies):
        @pl.when(me < n - 1)
        def _():
            copies[0].wait_send()

        @pl.when(me > 0)
        def _():
            copies[1].wait_send()

    off = off_ref[0]
    lane = lax.broadcasted_iota(jnp.int32, (rows, LANES), 1)
    row = lax.broadcasted_iota(jnp.int32, (rows, LANES), 0)
    gap = lane - row - off
    band = band_ref[...]
    rm = jnp.zeros((expo, rows, LANES), F32)
    for j in range(band.shape[2]):
        rm = rm + jnp.where((gap == j)[None], band[:, :, j:j + 1], 0.0)
    own = rm.reshape(er, LANES)
    moved = jnp.where((row < REACH)[None], pltpu.roll(own, rows, 1).reshape(rm.shape),
                      pltpu.roll(own, LANES - rows, 1).reshape(rm.shape))
    pk[:, :, 2 * wide:] = moved
    ra[0:er, :] = own
    flux = fl_ref[...]
    fx[rows:2 * rows, 0:fib] = flux

    pf[...] = jnp.zeros_like(pf)
    st[...] = jnp.zeros_like(st)
    pf[4:4 + pr_ref.shape[1], 0:fib] = pr_ref[0]
    st[:, 0:fib] = st_ref[...] - PITCH * lax.broadcasted_iota(jnp.int32, (1, fib), 1)
    near = jnp.zeros((PITCH, wide), F32)
    far = jnp.zeros((PITCH, wide), F32)
    for shift in range(4):
        hit = jnp.broadcast_to(st[...], (PITCH, wide)) == shift
        near = near + jnp.where(hit, pf[4 - shift:12 - shift, :], 0.0)
        far = far + jnp.where(hit, pf[12 - shift:20 - shift, :], 0.0)
    near2, far2, both = near * near, far * far, near * pltpu.roll(far, 1, 1)

    pl.semaphore_wait(barrier, n - 1)
    flux_copies = pair(0, fl_ref.at[rows - REACH:rows], fbu, fl_ref.at[0:REACH], fbd)
    start(flux_copies)

    cube = (LANES, PITCH, LANES)
    depth = lax.broadcasted_iota(jnp.int32, cube, 0) - lax.broadcasted_iota(jnp.int32, cube, 2)
    on, after = depth == 0, depth == 1
    last = lax.broadcasted_iota(jnp.int32, (PITCH, LANES), 1) == LANES - 1

    def parts(value):
        hi = value.astype(BF16).astype(F32)
        return hi, value - hi

    def spread(a, b):
        rest = 0.0 if b is None else jnp.where(after, b[None], 0.0)
        return jnp.where(on, a[None], rest).reshape(LANES * PITCH, LANES).astype(BF16)

    def edge(b):
        top = jnp.where(last, b, 0.0)
        return jnp.concatenate([top, jnp.zeros((LANES - PITCH, LANES), F32)], axis=0).astype(BF16)

    for j in range(chunks):
        at = slice(j * LANES, (j + 1) * LANES)
        part = slice(j * span, (j + 1) * span)
        a2, b2, bo, an, bf = [parts(v[:, at]) for v in (near2, far2, both, near, far)]
        wrhs = [jnp.concatenate([spread(a2[i], b2[i]), spread(bo[i], None)], axis=1) for i in (0, 1)]
        frhs = [spread(an[i], bf[i]) for i in (0, 1)]
        for copy in loads(j):
            copy.wait()
        w = (iv[:, :, part] * (1.0 - mk[:, :, part].astype(F32))).reshape(er, span)
        wf = w * fr[:, :, part].reshape(er, span)
        w, wf = split(w), split(wf)
        got = dot3(w, wrhs)
        da[0:er, at] = got[:, 0:LANES]
        oa[0:er, at] = got[:, LANES:]
        g[:, at] = dot3(wf, frhs)
        if j > 0:
            prev = slice((j - 1) * LANES, j * LANES)
            b2, bf = [parts(v[:, prev]) for v in (far2, far)]
            da[0:er, prev] += dot3([v[:, 0:LANES] for v in w], [edge(v) for v in b2])
            g[:, prev] += dot3([v[:, 0:LANES] for v in wf], [edge(v) for v in bf])

    pk[:, :, 0:wide] = da[0:er, :].reshape(expo, rows, wide)
    pk[:, :, wide:2 * wide] = oa[0:er, :].reshape(expo, rows, wide)

    arrive(flux_copies)
    fx[rows - REACH:rows, 0:fib] = fbu[...]
    fx[2 * rows:2 * rows + REACH, 0:fib] = fbd[...]
    y = dot6(own, fx[...])
    own_t = own.T
    fo[0] = dot6(own_t, g[...] - tri(da[0:er, :], oa[0:er, :], y))
    fo[1] = dot6(own_t * own_t, da[0:er, :])
    fold_copies = pair(1, fo.at[:, 2 * rows:2 * rows + REACH], fiu, fo.at[:, rows - REACH:rows], fid)
    start(fold_copies)
    pack_copies = pair(2, pk.at[:, rows - REACH:rows], pku, pk.at[:, 0:REACH], pkd)
    start(pack_copies)

    arrive(fold_copies)
    res = fo[0, rows:2 * rows] - RIDGE * fx[rows:2 * rows, :] + jnp.concatenate([fiu[0], fid[0]], axis=0)
    diag = fo[1, rows:2 * rows] + RIDGE + jnp.concatenate([fiu[1], fid[1]], axis=0)
    inv = 1.0 / diag
    vs, us = [res * inv], []
    sums = [total(vs[0] * res)]
    v_copies = []
    ra_t = None
    for k in range(3):
        vx[k, rows:2 * rows] = vs[k]
        copies = pair(3 + k, vx.at[k, rows:2 * rows], vx.at[k, 0:rows],
                      vx.at[k, rows:2 * rows], vx.at[k, 2 * rows:3 * rows])
        start(copies)
        v_copies.append(copies)
        if k == 0:
            arrive(pack_copies)
            side = expo * REACH
            for i, ref in ((0, pku), (1, pkd)):
                place = slice(er + i * side, er + (i + 1) * side)
                da[place, :] = ref[:, :, 0:wide].reshape(side, wide)
                oa[place, :] = ref[:, :, wide:2 * wide].reshape(side, wide)
                ra[place, :] = ref[:, :, 2 * wide:].reshape(side, LANES)
            ra_t = ra[...].T[rows:2 * rows]
        arrive(copies)
        y = tri(da[...], oa[...], dot6(ra[...], vx[k]))
        us.append(dot6(ra_t, y) + RIDGE * vs[k])
        if k < 2:
            vs.append(us[k] * inv - SHIFTS[k] * vs[k])
            sums.append(total(vs[k + 1] * res))
    for i in range(3):
        for k in range(i, 3):
            sums.append(total(vs[i] * us[k]))

    spot = lax.broadcasted_iota(jnp.int32, (1, LANES), 1)
    mine = jnp.zeros((1, LANES), F32)
    for i, s in enumerate(sums):
        mine = jnp.where(spot == i, s, mine)
    gown[...] = mine
    gall[me] = mine

    def push(d):
        return pltpu.make_async_remote_copy(
            src_ref=gown, dst_ref=gall.at[me], send_sem=gs.at[d], recv_sem=gr.at[d],
            device_id={"wave": lax.rem(me + d, n)}, device_id_type=pl.DeviceIdType.MESH)

    @pl.loop(1, n)
    def _(d):
        push(d).start()

    @pl.loop(1, n)
    def _(d):
        push(d).wait_recv()

    whole = jnp.sum(gall[...], axis=0)
    b0, b1, b2, a00, a01, a02, a11, a12, a22 = [
        total(jnp.where(spot == i, whole, 0.0)) for i in range(9)]
    l10, l20 = a01 / a00, a02 / a00
    d1, e21 = a11 - l10 * a01, a12 - l20 * a01
    l21 = e21 / d1
    d2 = a22 - l20 * a02 - l21 * e21
    y1 = b1 - l10 * b0
    y2 = b2 - l20 * b0 - l21 * y1
    c2 = y2 / d2
    c1 = y1 / d1 - l21 * c2
    c0 = b0 / a00 - l10 * c1 - l20 * c2
    new_x = fx[rows:2 * rows, :] + (c0 * vs[0] + c1 * vs[1] + c2 * vs[2])
    new_r = res - (c0 * us[0] + c1 * us[1] + c2 * us[2])
    x_ref[...] = new_x[:, 0:fib]
    r_ref[...] = new_r[:, 0:fib]

    for copies in [flux_copies, fold_copies, pack_copies] + v_copies:
        sent(copies)

    @pl.loop(1, n)
    def _(d):
        push(d).wait_send()


def solution(mesh):
    n = mesh.shape["wave"]

    def local(frames, inverse_var, masked, psf_band, offsets, starts, profile, flux_start):
        expo, rows, cols = frames.shape
        fib = flux_start.shape[1]
        chunks = -(-fib // LANES)
        wide = chunks * LANES
        er, side = expo * rows, expo * REACH
        vmem, smem = pl.BlockSpec(memory_space=pltpu.VMEM), pl.BlockSpec(memory_space=pltpu.SMEM)
        far = pl.BlockSpec(memory_space=pl.ANY)
        out = jax.ShapeDtypeStruct(flux_start.shape, F32)
        dma = pltpu.SemaphoreType.DMA
        frame = (expo, rows, cols)
        return pl.pallas_call(
            functools.partial(kernel, n, chunks=chunks),
            out_shape=(out, out),
            in_specs=[far, far, far, vmem, smem, vmem, vmem, vmem],
            out_specs=(vmem, vmem),
            scratch_shapes=[
                pltpu.VMEM(frame, F32), pltpu.VMEM(frame, F32), pltpu.VMEM(frame, jnp.int32),
                pltpu.VMEM((24, wide), F32), pltpu.VMEM((1, wide), jnp.int32),
                pltpu.VMEM((expo, rows, 2 * wide + LANES), F32), pltpu.VMEM((er, wide), F32),
                pltpu.VMEM((LANES, wide), F32), pltpu.VMEM((REACH, fib), F32), pltpu.VMEM((REACH, fib), F32),
                pltpu.VMEM((expo, REACH, 2 * wide + LANES), F32), pltpu.VMEM((expo, REACH, 2 * wide + LANES), F32),
                pltpu.VMEM((2, LANES, wide), F32), pltpu.VMEM((2, REACH, wide), F32), pltpu.VMEM((2, REACH, wide), F32),
                pltpu.VMEM((3, LANES, wide), F32), pltpu.VMEM((er + 2 * side, LANES), F32),
                pltpu.VMEM((er + 2 * side, wide), F32), pltpu.VMEM((er + 2 * side, wide), F32),
                pltpu.VMEM((1, LANES), F32), pltpu.VMEM((n, 1, LANES), F32),
                dma((3, chunks)), dma((6,)), dma((6,)), dma((6,)), dma((6,)), dma((n,)), dma((n,)),
            ],
            compiler_params=pltpu.CompilerParams(
                collective_id=0, has_side_effects=True, vmem_limit_bytes=56 * 1024 * 1024),
        )(frames, inverse_var, masked, psf_band, offsets, starts, profile, flux_start)

    frame = P(None, ("tile", "wave"), None)
    flat = P(("tile", "wave"), None)
    return jax.shard_map(
        local, mesh=mesh,
        in_specs=(frame, frame, frame, frame, P(("tile", "wave")), flat, P(("tile", "wave"), None, None), flat),
        out_specs=(flat, flat), check_vma=False)
```

```python
import functools

import jax
import jax.numpy as jnp
from jax import lax
from jax.experimental import pallas as pl
from jax.experimental.pallas import tpu as pltpu
from jax.sharding import PartitionSpec as P

RIDGE = 0.2
REACH = 16
PITCH = 8
LANES = 128
SHIFTS = (6.0, 2.0)
F32, BF16 = jnp.float32, jnp.bfloat16
HIGH = lax.Precision.HIGHEST


def dot6(a, b):
    return jnp.dot(a, b, precision=HIGH, preferred_element_type=F32)


def total(value):
    return jnp.sum(value, keepdims=True)


def tri(d, o, y):
    wide = y.shape[1]
    return d * y + o * pltpu.roll(y, 1, 1) + pltpu.roll(o * y, wide - 1, 1)


def kernel(n, fr_hbm, iv_hbm, mk_hbm, band_ref, off_ref, st_ref, pr_ref, fl_ref, x_ref, r_ref,
           fr, iv, mk, pf, st, nr, fr2, acc, pk, rs, g, fx, fbu, fbd, pku, pkd, rsu, rsd, fo, fiu, fid, vx, ra, da, oa, gown, gall,
           load, su, sd, ru, rd, gs, gr, *, chunks):
    expo, rows, cols = fr.shape
    fib = fl_ref.shape[1]
    wide = fx.shape[1]
    er = expo * rows
    span = cols // chunks
    me = lax.axis_index("wave")

    def loads(j):
        part = pl.ds(j * span, span)
        return [
            pltpu.make_async_copy(h.at[:, :, part], v.at[:, :, part], load.at[i, j])
            for i, (h, v) in enumerate(((iv_hbm, iv), (mk_hbm, mk), (fr_hbm, fr)))
        ]

    for j in reversed(range(chunks)):
        for copy in loads(j):
            copy.start()

    fx[...] = jnp.zeros_like(fx)
    fbu[...] = jnp.zeros_like(fbu)
    fbd[...] = jnp.zeros_like(fbd)
    pku[...] = jnp.zeros_like(pku)
    pkd[...] = jnp.zeros_like(pkd)
    rsu[...] = jnp.zeros_like(rsu)
    rsd[...] = jnp.zeros_like(rsd)
    fiu[...] = jnp.zeros_like(fiu)
    fid[...] = jnp.zeros_like(fid)
    vx[...] = jnp.zeros_like(vx)

    barrier = pltpu.get_barrier_semaphore()

    @pl.loop(1, n)
    def _(d):
        pl.semaphore_signal(barrier, inc=1, device_id={"wave": lax.rem(me + d, n)},
                            device_id_type=pl.DeviceIdType.MESH)

    def pair(k, down_src, down_dst, up_src, up_dst):
        down = pltpu.make_async_remote_copy(
            src_ref=down_src, dst_ref=down_dst, send_sem=sd.at[k], recv_sem=rd.at[k],
            device_id={"wave": lax.rem(me + 1, n)}, device_id_type=pl.DeviceIdType.MESH)
        up = pltpu.make_async_remote_copy(
            src_ref=up_src, dst_ref=up_dst, send_sem=su.at[k], recv_sem=ru.at[k],
            device_id={"wave": lax.rem(me + n - 1, n)}, device_id_type=pl.DeviceIdType.MESH)
        return down, up

    def start(copies):
        @pl.when(me < n - 1)
        def _():
            copies[0].start()

        @pl.when(me > 0)
        def _():
            copies[1].start()

    def arrive(copies):
        @pl.when(me > 0)
        def _():
            copies[0].wait_recv()

        @pl.when(me < n - 1)
        def _():
            copies[1].wait_recv()

    def sent(copies):
        @pl.when(me < n - 1)
        def _():
            copies[0].wait_send()

        @pl.when(me > 0)
        def _():
            copies[1].wait_send()

    off = off_ref[0]
    place = lax.broadcasted_iota(jnp.int32, (LANES, er), 0)
    row = lax.broadcasted_iota(jnp.int32, (LANES, er), 1) % rows
    gap = place - row - off
    band = jnp.concatenate([band_ref[e] for e in range(expo)], axis=1)
    own_t = jnp.zeros((LANES, er), F32)
    for j in range(band.shape[0]):
        own_t = own_t + jnp.where(gap == j, band[j:j + 1], 0.0)
    own = own_t.T
    ra[0:er, :] = own
    low = lax.broadcasted_iota(jnp.int32, (er, LANES), 0) % rows < REACH
    moved = jnp.where(low, pltpu.roll(own, rows, 1), pltpu.roll(own, LANES - rows, 1))
    rs[...] = moved.reshape(expo, rows, LANES)
    flux = fl_ref[...]
    fx[rows:2 * rows, 0:fib] = flux

    pf[...] = jnp.zeros_like(pf)
    st[...] = jnp.zeros_like(st)
    for p in range(pr_ref.shape[0]):
        pf[4 + p:5 + p, 0:fib] = pr_ref[p]
    st[:, 0:fib] = st_ref[...] - PITCH * lax.broadcasted_iota(jnp.int32, (1, fib), 1)
    near = jnp.zeros((PITCH, wide), F32)
    far = jnp.zeros((PITCH, wide), F32)
    for shift in range(4):
        hit = jnp.broadcast_to(st[...], (PITCH, wide)) == shift
        near = near + jnp.where(hit, pf[4 - shift:12 - shift, :], 0.0)
        far = far + jnp.where(hit, pf[12 - shift:20 - shift, :], 0.0)

    def lay(ref, value):
        ref[0:PITCH] = jnp.zeros((PITCH, LANES), F32)
        for j in range(chunks):
            block = value[:, j * LANES:(j + 1) * LANES]
            ref[PITCH + j * LANES:PITCH + (j + 1) * LANES] = jnp.concatenate([block] * (LANES // PITCH), axis=0).T

    lay(nr, near)
    lay(fr2, far)
    acc[...] = jnp.zeros_like(acc)

    pl.semaphore_wait(barrier, n - 1)
    flux_copies = pair(0, fl_ref.at[rows - REACH:rows], fbu, fl_ref.at[0:REACH], fbd)
    start(flux_copies)

    row_copies = pair(2, rs.at[:, rows - REACH:rows], rsu, rs.at[:, 0:REACH], rsd)
    start(row_copies)

    tile = 2 * LANES
    group = tile // PITCH
    height = group + PITCH
    line = lax.broadcasted_iota(jnp.int32, (height, tile), 0) - PITCH
    mark = lax.broadcasted_iota(jnp.int32, (height, tile), 1) // PITCH
    on, after = mark == line, mark == line + 1

    def spread(a, b):
        value = jnp.where(on, jnp.concatenate([a, a], axis=1), 0.0)
        if b is not None:
            value = jnp.where(after, jnp.concatenate([b, b], axis=1), value)
        hi = value.astype(BF16).astype(F32)
        return [hi, value - hi]

    def narrow(blocks, weights):
        left = jnp.concatenate(blocks, axis=0).astype(BF16)
        hi = weights.astype(BF16)
        right = jnp.concatenate([hi, (weights - hi.astype(F32)).astype(BF16)], axis=0)
        out = lax.dot_general(left, right, (((1,), (1,)), ((), ())), preferred_element_type=F32)
        half = len(blocks) * height // 2
        return out[0:half, 0:er] + (out[0:half, er:] + out[half:, 0:er])

    pack_copies = []
    for j in reversed(range(chunks)):
        for copy in loads(j):
            copy.wait()
        for t in reversed(range(j * span // tile, (j + 1) * span // tile)):
            part = slice(t * tile, (t + 1) * tile)
            at = slice(t * group, t * group + height)
            an, bf = nr[at], fr2[at]
            before = fr2[t * group + PITCH - 1:t * group + height - 1]
            before = jnp.concatenate([jnp.zeros((PITCH, LANES), F32), before], axis=0)
            w = (iv[:, :, part] * (1.0 - mk[:, :, part].astype(F32))).reshape(er, tile)
            d_hi, d_lo = spread(an * an, bf * bf)
            o_hi, o_lo = spread(an * before, None)
            c_hi, c_lo = spread(an, bf)
            got = narrow([d_hi, o_hi, d_lo, o_lo], w)
            acc[0, at] += got[0:height]
            acc[1, at] += got[height:]
            acc[2, at] += narrow([c_hi, c_lo], w * fr[:, :, part].reshape(er, tile))
        lanes = slice(j * LANES, (j + 1) * LANES)
        done = slice(PITCH + j * LANES, PITCH + (j + 1) * LANES)
        d, o = acc[0, done].T, acc[1, done].T
        da[0:er, lanes] = d
        oa[0:er, lanes] = o
        g[:, lanes] = acc[2, done].T
        pk[j, :, :, 0:LANES] = d.reshape(expo, rows, LANES)
        pk[j, :, :, LANES:] = o.reshape(expo, rows, LANES)
        copies = pair(6 + j, pk.at[j, :, rows - REACH:rows], pku.at[j], pk.at[j, :, 0:REACH], pkd.at[j])
        start(copies)
        pack_copies.append(copies)

    arrive(flux_copies)
    fx[rows - REACH:rows, 0:fib] = fbu[...]
    fx[2 * rows:2 * rows + REACH, 0:fib] = fbd[...]
    y = dot6(own, fx[...])
    fo[0] = dot6(own_t, g[...] - tri(da[0:er, :], oa[0:er, :], y))
    fo[1] = dot6(own_t * own_t, da[0:er, :])
    fold_copies = pair(1, fo.at[:, 2 * rows:2 * rows + REACH], fiu, fo.at[:, rows - REACH:rows], fid)
    start(fold_copies)
    arrive(fold_copies)
    res = fo[0, rows:2 * rows] - RIDGE * fx[rows:2 * rows, :] + jnp.concatenate([fiu[0], fid[0]], axis=0)
    diag = fo[1, rows:2 * rows] + RIDGE + jnp.concatenate([fiu[1], fid[1]], axis=0)
    inv = 1.0 / diag
    vs, us = [res * inv], []
    sums = [total(vs[0] * res)]
    v_copies = []
    ra_t = None
    for k in range(3):
        vx[k, rows:2 * rows] = vs[k]
        copies = pair(3 + k, vx.at[k, rows:2 * rows], vx.at[k, 0:rows],
                      vx.at[k, rows:2 * rows], vx.at[k, 2 * rows:3 * rows])
        start(copies)
        v_copies.append(copies)
        if k == 0:
            for each in [row_copies] + pack_copies:
                arrive(each)
            side = expo * REACH
            for i, (ref, rowref) in enumerate(((pku, rsu), (pkd, rsd))):
                place = slice(er + i * side, er + (i + 1) * side)
                ra[place, :] = rowref[...].reshape(side, LANES)
                for j in range(chunks):
                    lanes = slice(j * LANES, (j + 1) * LANES)
                    da[place, lanes] = ref[j, :, :, 0:LANES].reshape(side, LANES)
                    oa[place, lanes] = ref[j, :, :, LANES:].reshape(side, LANES)
            ra_t = ra[...].T[rows:2 * rows]
        arrive(copies)
        y = tri(da[...], oa[...], dot6(ra[...], vx[k]))
        us.append(dot6(ra_t, y) + RIDGE * vs[k])
        if k < 2:
            vs.append(us[k] * inv - SHIFTS[k] * vs[k])
            sums.append(total(vs[k + 1] * res))
    for i in range(3):
        for k in range(i, 3):
            sums.append(total(vs[i] * us[k]))

    spot = lax.broadcasted_iota(jnp.int32, (1, LANES), 1)
    mine = jnp.zeros((1, LANES), F32)
    for i, s in enumerate(sums):
        mine = jnp.where(spot == i, s, mine)
    gown[...] = mine
    gall[me] = mine

    def push(d):
        return pltpu.make_async_remote_copy(
            src_ref=gown, dst_ref=gall.at[me], send_sem=gs.at[d], recv_sem=gr.at[d],
            device_id={"wave": lax.rem(me + d, n)}, device_id_type=pl.DeviceIdType.MESH)

    @pl.loop(1, n)
    def _(d):
        push(d).start()

    @pl.loop(1, n)
    def _(d):
        push(d).wait_recv()

    whole = jnp.sum(gall[...], axis=0)
    b0, b1, b2, a00, a01, a02, a11, a12, a22 = [
        total(jnp.where(spot == i, whole, 0.0)) for i in range(9)]
    l10, l20 = a01 / a00, a02 / a00
    d1, e21 = a11 - l10 * a01, a12 - l20 * a01
    l21 = e21 / d1
    d2 = a22 - l20 * a02 - l21 * e21
    y1 = b1 - l10 * b0
    y2 = b2 - l20 * b0 - l21 * y1
    c2 = y2 / d2
    c1 = y1 / d1 - l21 * c2
    c0 = b0 / a00 - l10 * c1 - l20 * c2
    new_x = fx[rows:2 * rows, :] + (c0 * vs[0] + c1 * vs[1] + c2 * vs[2])
    new_r = res - (c0 * us[0] + c1 * us[1] + c2 * us[2])
    x_ref[...] = new_x[:, 0:fib]
    r_ref[...] = new_r[:, 0:fib]

    for copies in [flux_copies, fold_copies, row_copies] + pack_copies + v_copies:
        sent(copies)

    @pl.loop(1, n)
    def _(d):
        push(d).wait_send()


def hand_over(x_ref, r_ref, x_out, r_out):
    x_out[...] = x_ref[...]
    r_out[...] = r_ref[...]


def solution(mesh):
    n = mesh.shape["wave"]

    def local(frames, inverse_var, masked, psf_band, offsets, starts, profile, flux_start):
        expo, rows, cols = frames.shape
        fib = flux_start.shape[1]
        chunks = -(-fib // LANES)
        wide = chunks * LANES
        er, side = expo * rows, expo * REACH
        vmem, smem = pl.BlockSpec(memory_space=pltpu.VMEM), pl.BlockSpec(memory_space=pltpu.SMEM)
        far = pl.BlockSpec(memory_space=pl.ANY)
        out = jax.ShapeDtypeStruct(flux_start.shape, F32)
        dma = pltpu.SemaphoreType.DMA
        frame = (expo, rows, cols)
        found = pl.pallas_call(
            functools.partial(kernel, n, chunks=chunks),
            out_shape=(out, out),
            in_specs=[far, far, far, vmem, smem, vmem, vmem, vmem],
            out_specs=(vmem, vmem),
            scratch_shapes=[
                pltpu.VMEM(frame, F32), pltpu.VMEM(frame, F32), pltpu.VMEM(frame, jnp.int32),
                pltpu.VMEM((24, wide), F32), pltpu.VMEM((1, wide), jnp.int32),
                pltpu.VMEM((wide + PITCH, LANES), F32), pltpu.VMEM((wide + PITCH, LANES), F32),
                pltpu.VMEM((3, wide + PITCH, er), F32), pltpu.VMEM((chunks, expo, rows, 2 * LANES), F32),
                pltpu.VMEM((expo, rows, LANES), F32), pltpu.VMEM((er, wide), F32),
                pltpu.VMEM((LANES, wide), F32), pltpu.VMEM((REACH, fib), F32), pltpu.VMEM((REACH, fib), F32),
                pltpu.VMEM((chunks, expo, REACH, 2 * LANES), F32), pltpu.VMEM((chunks, expo, REACH, 2 * LANES), F32),
                pltpu.VMEM((expo, REACH, LANES), F32), pltpu.VMEM((expo, REACH, LANES), F32),
                pltpu.VMEM((2, LANES, wide), F32), pltpu.VMEM((2, REACH, wide), F32), pltpu.VMEM((2, REACH, wide), F32),
                pltpu.VMEM((3, LANES, wide), F32), pltpu.VMEM((er + 2 * side, LANES), F32),
                pltpu.VMEM((er + 2 * side, wide), F32), pltpu.VMEM((er + 2 * side, wide), F32),
                pltpu.VMEM((1, LANES), F32), pltpu.VMEM((n, 1, LANES), F32),
                dma((3, chunks)), *[dma((6 + chunks,))] * 4, dma((n,)), dma((n,)),
            ],
            compiler_params=pltpu.CompilerParams(
                collective_id=0, has_side_effects=True, vmem_limit_bytes=56 * 1024 * 1024),
        )(frames, inverse_var, masked, jnp.swapaxes(psf_band, 1, 2), offsets, starts,
          jnp.swapaxes(profile, 0, 1), flux_start)
        return pl.pallas_call(hand_over, out_shape=(out, out), in_specs=[vmem, vmem], out_specs=(vmem, vmem))(*found)

    frame = P(None, ("tile", "wave"), None)
    flat = P(("tile", "wave"), None)
    return jax.shard_map(
        local, mesh=mesh,
        in_specs=(frame, frame, frame, frame, P(("tile", "wave")), flat, P(("tile", "wave"), None, None), flat),
        out_specs=(flat, flat), check_vma=False)
```

```python
import functools

import jax
import jax.numpy as jnp
from jax import lax
from jax.experimental import pallas as pl
from jax.experimental.pallas import tpu as pltpu
from jax.sharding import PartitionSpec as P

RIDGE = 0.2
REACH = 16
PITCH = 8
LANES = 128
SHIFTS = (6.0, 2.0)
F32, BF16 = jnp.float32, jnp.bfloat16
HIGH = lax.Precision.HIGHEST


def dot6(a, b):
    return jnp.dot(a, b, precision=HIGH, preferred_element_type=F32)


def total(value):
    return jnp.sum(value, keepdims=True)


def tri(d, o, y):
    wide = y.shape[1]
    return d * y + o * pltpu.roll(y, 1, 1) + pltpu.roll(o * y, wide - 1, 1)


def kernel(n, fr_hbm, iv_hbm, mk_hbm, band_ref, off_ref, st_ref, pr_ref, fl_ref, x_ref, r_ref,
           fr, iv, mk, pf, st, nr, fr2, acc, pk, rs, g, fx, fbu, fbd, pku, pkd, rsu, rsd, fo, fiu, fid, vx, ra, da, oa, gown, gall,
           load, su, sd, ru, rd, gs, gr, *, chunks):
    expo, rows, cols = fr.shape
    fib = fl_ref.shape[1]
    wide = fx.shape[1]
    er = expo * rows
    span = cols // chunks
    me = lax.axis_index("wave")

    def loads(j):
        part = pl.ds(j * span, span)
        return [
            pltpu.make_async_copy(h.at[:, :, part], v.at[:, :, part], load.at[i, j])
            for i, (h, v) in enumerate(((iv_hbm, iv), (mk_hbm, mk), (fr_hbm, fr)))
        ]

    for j in reversed(range(chunks)):
        for copy in loads(j):
            copy.start()

    fx[...] = jnp.zeros_like(fx)
    fbu[...] = jnp.zeros_like(fbu)
    fbd[...] = jnp.zeros_like(fbd)
    pku[...] = jnp.zeros_like(pku)
    pkd[...] = jnp.zeros_like(pkd)
    rsu[...] = jnp.zeros_like(rsu)
    rsd[...] = jnp.zeros_like(rsd)
    fiu[...] = jnp.zeros_like(fiu)
    fid[...] = jnp.zeros_like(fid)
    vx[...] = jnp.zeros_like(vx)

    barrier = pltpu.get_barrier_semaphore()

    @pl.loop(1, n)
    def _(d):
        pl.semaphore_signal(barrier, inc=1, device_id={"wave": lax.rem(me + d, n)},
                            device_id_type=pl.DeviceIdType.MESH)

    def pair(k, down_src, down_dst, up_src, up_dst):
        down = pltpu.make_async_remote_copy(
            src_ref=down_src, dst_ref=down_dst, send_sem=sd.at[k], recv_sem=rd.at[k],
            device_id={"wave": lax.rem(me + 1, n)}, device_id_type=pl.DeviceIdType.MESH)
        up = pltpu.make_async_remote_copy(
            src_ref=up_src, dst_ref=up_dst, send_sem=su.at[k], recv_sem=ru.at[k],
            device_id={"wave": lax.rem(me + n - 1, n)}, device_id_type=pl.DeviceIdType.MESH)
        return down, up

    def start(copies):
        @pl.when(me < n - 1)
        def _():
            copies[0].start()

        @pl.when(me > 0)
        def _():
            copies[1].start()

    def arrive(copies):
        @pl.when(me > 0)
        def _():
            copies[0].wait_recv()

        @pl.when(me < n - 1)
        def _():
            copies[1].wait_recv()

    def sent(copies):
        @pl.when(me < n - 1)
        def _():
            copies[0].wait_send()

        @pl.when(me > 0)
        def _():
            copies[1].wait_send()

    off = off_ref[0]
    place = lax.broadcasted_iota(jnp.int32, (LANES, er), 0)
    row = lax.broadcasted_iota(jnp.int32, (LANES, er), 1) % rows
    gap = place - row - off
    band = jnp.concatenate([band_ref[e] for e in range(expo)], axis=1)
    own_t = jnp.zeros((LANES, er), F32)
    for j in range(band.shape[0]):
        own_t = own_t + jnp.where(gap == j, band[j:j + 1], 0.0)
    own = own_t.T
    ra[0:er, :] = own
    low = lax.broadcasted_iota(jnp.int32, (er, LANES), 0) % rows < REACH
    moved = jnp.where(low, pltpu.roll(own, rows, 1), pltpu.roll(own, LANES - rows, 1))
    rs[...] = moved.reshape(expo, rows, LANES)
    flux = fl_ref[...]
    fx[rows:2 * rows, 0:fib] = flux

    pf[...] = jnp.zeros_like(pf)
    st[...] = jnp.zeros_like(st)
    for p in range(pr_ref.shape[0]):
        pf[4 + p:5 + p, 0:fib] = pr_ref[p]
    st[:, 0:fib] = st_ref[...] - PITCH * lax.broadcasted_iota(jnp.int32, (1, fib), 1)
    near = jnp.zeros((PITCH, wide), F32)
    far = jnp.zeros((PITCH, wide), F32)
    for shift in range(4):
        hit = jnp.broadcast_to(st[...], (PITCH, wide)) == shift
        near = near + jnp.where(hit, pf[4 - shift:12 - shift, :], 0.0)
        far = far + jnp.where(hit, pf[12 - shift:20 - shift, :], 0.0)

    def lay(ref, value):
        ref[0:PITCH] = jnp.zeros((PITCH, LANES), F32)
        for j in range(chunks):
            block = value[:, j * LANES:(j + 1) * LANES]
            ref[PITCH + j * LANES:PITCH + (j + 1) * LANES] = jnp.concatenate([block] * (LANES // PITCH), axis=0).T

    lay(nr, near)
    lay(fr2, far)
    acc[...] = jnp.zeros_like(acc)

    pl.semaphore_wait(barrier, n - 1)
    flux_copies = pair(0, fl_ref.at[rows - REACH:rows], fbu, fl_ref.at[0:REACH], fbd)
    start(flux_copies)

    row_copies = pair(2, rs.at[:, rows - REACH:rows], rsu, rs.at[:, 0:REACH], rsd)
    start(row_copies)

    tile = 2 * LANES
    group = tile // PITCH
    height = group + PITCH
    line = lax.broadcasted_iota(jnp.int32, (height, tile), 0) - PITCH
    mark = lax.broadcasted_iota(jnp.int32, (height, tile), 1) // PITCH
    on, after = mark == line, mark == line + 1

    def spread(a, b):
        value = jnp.where(on, jnp.concatenate([a, a], axis=1), 0.0)
        if b is not None:
            value = jnp.where(after, jnp.concatenate([b, b], axis=1), value)
        hi = value.astype(BF16).astype(F32)
        return [hi, value - hi]

    def narrow(blocks, weights):
        left = jnp.concatenate(blocks, axis=0).astype(BF16)
        hi = weights.astype(BF16)
        right = jnp.concatenate([hi, (weights - hi.astype(F32)).astype(BF16)], axis=0)
        out = lax.dot_general(left, right, (((1,), (1,)), ((), ())), preferred_element_type=F32)
        half = len(blocks) * height // 2
        return out[0:half, 0:er] + (out[0:half, er:] + out[half:, 0:er])

    pack_copies = []
    for j in reversed(range(chunks)):
        for copy in loads(j):
            copy.wait()
        for t in reversed(range(j * span // tile, (j + 1) * span // tile)):
            part = slice(t * tile, (t + 1) * tile)
            at = slice(t * group, t * group + height)
            an, bf = nr[at], fr2[at]
            before = fr2[t * group + PITCH - 1:t * group + height - 1]
            before = jnp.concatenate([jnp.zeros((PITCH, LANES), F32), before], axis=0)
            w = (iv[:, :, part] * (1.0 - mk[:, :, part].astype(F32))).reshape(er, tile)
            d_hi, d_lo = spread(an * an, bf * bf)
            o_hi, o_lo = spread(an * before, None)
            c_hi, c_lo = spread(an, bf)
            got = narrow([d_hi, o_hi, d_lo, o_lo], w)
            acc[0, at] += got[0:height]
            acc[1, at] += got[height:]
            acc[2, at] += narrow([c_hi, c_lo], w * fr[:, :, part].reshape(er, tile))
        lanes = slice(j * LANES, (j + 1) * LANES)
        done = slice(PITCH + j * LANES, PITCH + (j + 1) * LANES)
        d, o = acc[0, done].T, acc[1, done].T
        da[0:er, lanes] = d
        oa[0:er, lanes] = o
        g[:, lanes] = acc[2, done].T
        pk[j, :, :, 0:LANES] = d.reshape(expo, rows, LANES)
        pk[j, :, :, LANES:] = o.reshape(expo, rows, LANES)
        copies = pair(6 + j, pk.at[j, :, rows - REACH:rows], pku.at[j], pk.at[j, :, 0:REACH], pkd.at[j])
        if j > 0:
            start(copies)
        pack_copies.append(copies)

    arrive(flux_copies)
    fx[rows - REACH:rows, 0:fib] = fbu[...]
    fx[2 * rows:2 * rows + REACH, 0:fib] = fbd[...]
    y = dot6(own, fx[...])
    fo[0] = dot6(own_t, g[...] - tri(da[0:er, :], oa[0:er, :], y))
    fo[1] = dot6(own_t * own_t, da[0:er, :])
    fold_copies = pair(1, fo.at[:, 2 * rows:2 * rows + REACH], fiu, fo.at[:, rows - REACH:rows], fid)
    start(fold_copies)
    start(pack_copies[-1])
    arrive(fold_copies)
    res = fo[0, rows:2 * rows] - RIDGE * fx[rows:2 * rows, :] + jnp.concatenate([fiu[0], fid[0]], axis=0)
    diag = fo[1, rows:2 * rows] + RIDGE + jnp.concatenate([fiu[1], fid[1]], axis=0)
    inv = 1.0 / diag
    vs, us = [res * inv], []
    sums = [total(vs[0] * res)]
    v_copies = []
    ra_t = None
    for k in range(3):
        vx[k, rows:2 * rows] = vs[k]
        copies = pair(3 + k, vx.at[k, rows:2 * rows], vx.at[k, 0:rows],
                      vx.at[k, rows:2 * rows], vx.at[k, 2 * rows:3 * rows])
        start(copies)
        v_copies.append(copies)
        if k == 0:
            for each in [row_copies] + pack_copies:
                arrive(each)
            side = expo * REACH
            for i, (ref, rowref) in enumerate(((pku, rsu), (pkd, rsd))):
                place = slice(er + i * side, er + (i + 1) * side)
                ra[place, :] = rowref[...].reshape(side, LANES)
                for j in range(chunks):
                    lanes = slice(j * LANES, (j + 1) * LANES)
                    da[place, lanes] = ref[j, :, :, 0:LANES].reshape(side, LANES)
                    oa[place, lanes] = ref[j, :, :, LANES:].reshape(side, LANES)
            ra_t = ra[...].T[rows:2 * rows]
        arrive(copies)
        image = dot6(ra[...], vx[k])
        y = tri(da[...], oa[...], image)
        if k < 2:
            us.append(dot6(ra_t, y) + RIDGE * vs[k])
            vs.append(us[k] * inv - SHIFTS[k] * vs[k])
            sums.append(total(vs[k + 1] * res))
    for i in range(2):
        for k in range(i, 2):
            sums.append(total(vs[i] * us[k]))
        sums.append(total(us[i] * vs[2]))
    sums.append(total(image[0:er] * y[0:er]) + RIDGE * total(vs[2] * vs[2]))

    spot = lax.broadcasted_iota(jnp.int32, (1, LANES), 1)
    mine = jnp.zeros((1, LANES), F32)
    for i, s in enumerate(sums):
        mine = jnp.where(spot == i, s, mine)
    gown[...] = mine
    gall[me] = mine

    def push(d):
        return pltpu.make_async_remote_copy(
            src_ref=gown, dst_ref=gall.at[me], send_sem=gs.at[d], recv_sem=gr.at[d],
            device_id={"wave": lax.rem(me + d, n)}, device_id_type=pl.DeviceIdType.MESH)

    @pl.loop(1, n)
    def _(d):
        push(d).start()

    us.append(dot6(ra_t, y) + RIDGE * vs[2])

    @pl.loop(1, n)
    def _(d):
        push(d).wait_recv()

    whole = jnp.sum(gall[...], axis=0)
    b0, b1, b2, a00, a01, a02, a11, a12, a22 = [
        total(jnp.where(spot == i, whole, 0.0)) for i in range(9)]
    l10, l20 = a01 / a00, a02 / a00
    d1, e21 = a11 - l10 * a01, a12 - l20 * a01
    l21 = e21 / d1
    d2 = a22 - l20 * a02 - l21 * e21
    y1 = b1 - l10 * b0
    y2 = b2 - l20 * b0 - l21 * y1
    c2 = y2 / d2
    c1 = y1 / d1 - l21 * c2
    c0 = b0 / a00 - l10 * c1 - l20 * c2
    new_x = fx[rows:2 * rows, :] + (c0 * vs[0] + c1 * vs[1] + c2 * vs[2])
    new_r = res - (c0 * us[0] + c1 * us[1] + c2 * us[2])
    x_ref[...] = new_x[:, 0:fib]
    r_ref[...] = new_r[:, 0:fib]

    for copies in [flux_copies, fold_copies, row_copies] + pack_copies + v_copies:
        sent(copies)

    @pl.loop(1, n)
    def _(d):
        push(d).wait_send()


def hand_over(x_ref, r_ref, x_out, r_out):
    x_out[...] = x_ref[...]
    r_out[...] = r_ref[...]


def solution(mesh):
    n = mesh.shape["wave"]

    def local(frames, inverse_var, masked, psf_band, offsets, starts, profile, flux_start):
        expo, rows, cols = frames.shape
        fib = flux_start.shape[1]
        chunks = -(-fib // LANES)
        wide = chunks * LANES
        er, side = expo * rows, expo * REACH
        vmem, smem = pl.BlockSpec(memory_space=pltpu.VMEM), pl.BlockSpec(memory_space=pltpu.SMEM)
        far = pl.BlockSpec(memory_space=pl.ANY)
        out = jax.ShapeDtypeStruct(flux_start.shape, F32)
        dma = pltpu.SemaphoreType.DMA
        frame = (expo, rows, cols)
        found = pl.pallas_call(
            functools.partial(kernel, n, chunks=chunks),
            out_shape=(out, out),
            in_specs=[far, far, far, vmem, smem, vmem, vmem, vmem],
            out_specs=(vmem, vmem),
            scratch_shapes=[
                pltpu.VMEM(frame, F32), pltpu.VMEM(frame, F32), pltpu.VMEM(frame, jnp.int32),
                pltpu.VMEM((24, wide), F32), pltpu.VMEM((1, wide), jnp.int32),
                pltpu.VMEM((wide + PITCH, LANES), F32), pltpu.VMEM((wide + PITCH, LANES), F32),
                pltpu.VMEM((3, wide + PITCH, er), F32), pltpu.VMEM((chunks, expo, rows, 2 * LANES), F32),
                pltpu.VMEM((expo, rows, LANES), F32), pltpu.VMEM((er, wide), F32),
                pltpu.VMEM((LANES, wide), F32), pltpu.VMEM((REACH, fib), F32), pltpu.VMEM((REACH, fib), F32),
                pltpu.VMEM((chunks, expo, REACH, 2 * LANES), F32), pltpu.VMEM((chunks, expo, REACH, 2 * LANES), F32),
                pltpu.VMEM((expo, REACH, LANES), F32), pltpu.VMEM((expo, REACH, LANES), F32),
                pltpu.VMEM((2, LANES, wide), F32), pltpu.VMEM((2, REACH, wide), F32), pltpu.VMEM((2, REACH, wide), F32),
                pltpu.VMEM((3, LANES, wide), F32), pltpu.VMEM((er + 2 * side, LANES), F32),
                pltpu.VMEM((er + 2 * side, wide), F32), pltpu.VMEM((er + 2 * side, wide), F32),
                pltpu.VMEM((1, LANES), F32), pltpu.VMEM((n, 1, LANES), F32),
                dma((3, chunks)), *[dma((6 + chunks,))] * 4, dma((n,)), dma((n,)),
            ],
            compiler_params=pltpu.CompilerParams(
                collective_id=0, has_side_effects=True, vmem_limit_bytes=56 * 1024 * 1024),
        )(frames, inverse_var, masked, jnp.swapaxes(psf_band, 1, 2), offsets, starts,
          jnp.swapaxes(profile, 0, 1), flux_start)
        return pl.pallas_call(hand_over, out_shape=(out, out), in_specs=[vmem, vmem], out_specs=(vmem, vmem))(*found)

    frame = P(None, ("tile", "wave"), None)
    flat = P(("tile", "wave"), None)
    return jax.shard_map(
        local, mesh=mesh,
        in_specs=(frame, frame, frame, frame, P(("tile", "wave")), flat, P(("tile", "wave"), None, None), flat),
        out_specs=(flat, flat), check_vma=False)
```

```python
import functools

import jax
import jax.numpy as jnp
from jax import lax
from jax.experimental import pallas as pl
from jax.experimental.pallas import tpu as pltpu
from jax.sharding import PartitionSpec as P

RIDGE = 0.2
REACH = 16
PITCH = 8
LANES = 128
SHIFTS = (6.0, 2.0)
F32, BF16 = jnp.float32, jnp.bfloat16
HIGH = lax.Precision.HIGHEST


def dot6(a, b):
    return jnp.dot(a, b, precision=HIGH, preferred_element_type=F32)


def dot(a, b):
    return jnp.dot(a, b, preferred_element_type=F32)


def split(value):
    hi = value.astype(BF16)
    return hi, (value - hi.astype(F32)).astype(BF16)


def dot3(a, b):
    return dot(a[0], b[0]) + (dot(a[1], b[0]) + dot(a[0], b[1]))


def total(value):
    return jnp.sum(value, keepdims=True)


def tri(d, o, y):
    wide = y.shape[1]
    return d * y + o * pltpu.roll(y, 1, 1) + pltpu.roll(o * y, wide - 1, 1)


def kernel(n, fr_hbm, iv_hbm, mk_hbm, band_ref, off_ref, st_ref, pr_ref, fl_ref, x_ref, r_ref,
           fr, iv, mk, pf, st, nr, fr2, acc, pk, rs, g, fx, fbu, fbd, pku, pkd, rsu, rsd, fo, fiu, fid, vx, ra, da, oa, gown, gall,
           load, su, sd, ru, rd, gs, gr, *, chunks):
    expo, rows, cols = fr.shape
    fib = fl_ref.shape[1]
    wide = fx.shape[1]
    er = expo * rows
    span = cols // chunks
    me = lax.axis_index("wave")

    def loads(j):
        part = pl.ds(j * span, span)
        return [
            pltpu.make_async_copy(h.at[:, :, part], v.at[:, :, part], load.at[i, j])
            for i, (h, v) in enumerate(((iv_hbm, iv), (mk_hbm, mk), (fr_hbm, fr)))
        ]

    for j in reversed(range(chunks)):
        for copy in loads(j):
            copy.start()

    fx[...] = jnp.zeros_like(fx)
    fbu[...] = jnp.zeros_like(fbu)
    fbd[...] = jnp.zeros_like(fbd)
    pku[...] = jnp.zeros_like(pku)
    pkd[...] = jnp.zeros_like(pkd)
    rsu[...] = jnp.zeros_like(rsu)
    rsd[...] = jnp.zeros_like(rsd)
    fiu[...] = jnp.zeros_like(fiu)
    fid[...] = jnp.zeros_like(fid)
    vx[...] = jnp.zeros_like(vx)

    barrier = pltpu.get_barrier_semaphore()

    @pl.loop(1, n)
    def _(d):
        pl.semaphore_signal(barrier, inc=1, device_id={"wave": lax.rem(me + d, n)},
                            device_id_type=pl.DeviceIdType.MESH)

    def pair(k, down_src, down_dst, up_src, up_dst):
        down = pltpu.make_async_remote_copy(
            src_ref=down_src, dst_ref=down_dst, send_sem=sd.at[k], recv_sem=rd.at[k],
            device_id={"wave": lax.rem(me + 1, n)}, device_id_type=pl.DeviceIdType.MESH)
        up = pltpu.make_async_remote_copy(
            src_ref=up_src, dst_ref=up_dst, send_sem=su.at[k], recv_sem=ru.at[k],
            device_id={"wave": lax.rem(me + n - 1, n)}, device_id_type=pl.DeviceIdType.MESH)
        return down, up

    def start(copies):
        @pl.when(me < n - 1)
        def _():
            copies[0].start()

        @pl.when(me > 0)
        def _():
            copies[1].start()

    def arrive(copies):
        @pl.when(me > 0)
        def _():
            copies[0].wait_recv()

        @pl.when(me < n - 1)
        def _():
            copies[1].wait_recv()

    def sent(copies):
        @pl.when(me < n - 1)
        def _():
            copies[0].wait_send()

        @pl.when(me > 0)
        def _():
            copies[1].wait_send()

    off = off_ref[0]
    place = lax.broadcasted_iota(jnp.int32, (LANES, er), 0)
    row = lax.broadcasted_iota(jnp.int32, (LANES, er), 1) % rows
    gap = place - row - off
    band = jnp.concatenate([band_ref[e] for e in range(expo)], axis=1)
    own_t = jnp.zeros((LANES, er), F32)
    for j in range(band.shape[0]):
        own_t = own_t + jnp.where(gap == j, band[j:j + 1], 0.0)
    own = own_t.T
    ra[0:er, :] = own
    low = lax.broadcasted_iota(jnp.int32, (er, LANES), 0) % rows < REACH
    moved = jnp.where(low, pltpu.roll(own, rows, 1), pltpu.roll(own, LANES - rows, 1))
    rs[...] = moved.reshape(expo, rows, LANES)
    flux = fl_ref[...]
    fx[rows:2 * rows, 0:fib] = flux

    pf[...] = jnp.zeros_like(pf)
    st[...] = jnp.zeros_like(st)
    for p in range(pr_ref.shape[0]):
        pf[4 + p:5 + p, 0:fib] = pr_ref[p]
    st[:, 0:fib] = st_ref[...] - PITCH * lax.broadcasted_iota(jnp.int32, (1, fib), 1)
    near = jnp.zeros((PITCH, wide), F32)
    far = jnp.zeros((PITCH, wide), F32)
    for shift in range(4):
        hit = jnp.broadcast_to(st[...], (PITCH, wide)) == shift
        near = near + jnp.where(hit, pf[4 - shift:12 - shift, :], 0.0)
        far = far + jnp.where(hit, pf[12 - shift:20 - shift, :], 0.0)

    def lay(ref, value):
        ref[0:PITCH] = jnp.zeros((PITCH, LANES), F32)
        for j in range(chunks):
            block = value[:, j * LANES:(j + 1) * LANES]
            ref[PITCH + j * LANES:PITCH + (j + 1) * LANES] = jnp.concatenate([block] * (LANES // PITCH), axis=0).T

    lay(nr, near)
    lay(fr2, far)
    acc[...] = jnp.zeros_like(acc)

    pl.semaphore_wait(barrier, n - 1)
    flux_copies = pair(0, fl_ref.at[rows - REACH:rows], fbu, fl_ref.at[0:REACH], fbd)
    start(flux_copies)

    row_copies = pair(2, rs.at[:, rows - REACH:rows], rsu, rs.at[:, 0:REACH], rsd)
    start(row_copies)

    tile = 2 * LANES
    group = tile // PITCH
    height = group + PITCH
    line = lax.broadcasted_iota(jnp.int32, (height, tile), 0) - PITCH
    mark = lax.broadcasted_iota(jnp.int32, (height, tile), 1) // PITCH
    on, after = mark == line, mark == line + 1

    def spread(a, b):
        value = jnp.where(on, jnp.concatenate([a, a], axis=1), 0.0)
        if b is not None:
            value = jnp.where(after, jnp.concatenate([b, b], axis=1), value)
        hi = value.astype(BF16).astype(F32)
        return [hi, value - hi]

    def narrow(blocks, weights):
        left = jnp.concatenate(blocks, axis=0).astype(BF16)
        hi = weights.astype(BF16)
        right = jnp.concatenate([hi, (weights - hi.astype(F32)).astype(BF16)], axis=0)
        out = lax.dot_general(left, right, (((1,), (1,)), ((), ())), preferred_element_type=F32)
        half = len(blocks) * height // 2
        return out[0:half, 0:er] + (out[0:half, er:] + out[half:, 0:er])

    pack_copies = []
    for j in reversed(range(chunks)):
        for copy in loads(j):
            copy.wait()
        for t in reversed(range(j * span // tile, (j + 1) * span // tile)):
            part = slice(t * tile, (t + 1) * tile)
            at = slice(t * group, t * group + height)
            an, bf = nr[at], fr2[at]
            before = fr2[t * group + PITCH - 1:t * group + height - 1]
            before = jnp.concatenate([jnp.zeros((PITCH, LANES), F32), before], axis=0)
            w = (iv[:, :, part] * (1.0 - mk[:, :, part].astype(F32))).reshape(er, tile)
            d_hi, d_lo = spread(an * an, bf * bf)
            o_hi, o_lo = spread(an * before, None)
            c_hi, c_lo = spread(an, bf)
            got = narrow([d_hi, o_hi, d_lo, o_lo], w)
            acc[0, at] += got[0:height]
            acc[1, at] += got[height:]
            acc[2, at] += narrow([c_hi, c_lo], w * fr[:, :, part].reshape(er, tile))
        lanes = slice(j * LANES, (j + 1) * LANES)
        done = slice(PITCH + j * LANES, PITCH + (j + 1) * LANES)
        d, o = acc[0, done].T, acc[1, done].T
        da[0:er, lanes] = d
        oa[0:er, lanes] = o
        g[:, lanes] = acc[2, done].T
        pk[j, :, :, 0:LANES] = d.reshape(expo, rows, LANES)
        pk[j, :, :, LANES:] = o.reshape(expo, rows, LANES)
        copies = pair(6 + j, pk.at[j, :, rows - REACH:rows], pku.at[j], pk.at[j, :, 0:REACH], pkd.at[j])
        if j > 0:
            start(copies)
        pack_copies.append(copies)

    arrive(flux_copies)
    fx[rows - REACH:rows, 0:fib] = fbu[...]
    fx[2 * rows:2 * rows + REACH, 0:fib] = fbd[...]
    y = dot6(own, fx[...])
    fo[0] = dot6(own_t, g[...] - tri(da[0:er, :], oa[0:er, :], y))
    fo[1] = dot6(own_t * own_t, da[0:er, :])
    fold_copies = pair(1, fo.at[:, 2 * rows:2 * rows + REACH], fiu, fo.at[:, rows - REACH:rows], fid)
    start(fold_copies)
    start(pack_copies[-1])
    arrive(fold_copies)
    res = fo[0, rows:2 * rows] - RIDGE * fx[rows:2 * rows, :] + jnp.concatenate([fiu[0], fid[0]], axis=0)
    diag = fo[1, rows:2 * rows] + RIDGE + jnp.concatenate([fiu[1], fid[1]], axis=0)
    inv = 1.0 / diag
    vs, us = [res * inv], []
    sums = [total(vs[0] * res)]
    v_copies = []
    ra_t = None
    for k in range(3):
        vx[k, rows:2 * rows] = vs[k]
        copies = pair(3 + k, vx.at[k, rows:2 * rows], vx.at[k, 0:rows],
                      vx.at[k, rows:2 * rows], vx.at[k, 2 * rows:3 * rows])
        start(copies)
        v_copies.append(copies)
        if k == 0:
            for each in [row_copies] + pack_copies:
                arrive(each)
            side = expo * REACH
            for i, (ref, rowref) in enumerate(((pku, rsu), (pkd, rsd))):
                place = slice(er + i * side, er + (i + 1) * side)
                ra[place, :] = rowref[...].reshape(side, LANES)
                for j in range(chunks):
                    lanes = slice(j * LANES, (j + 1) * LANES)
                    da[place, lanes] = ref[j, :, :, 0:LANES].reshape(side, LANES)
                    oa[place, lanes] = ref[j, :, :, LANES:].reshape(side, LANES)
            ra_s, ra_t = split(ra[...]), split(ra[...].T[rows:2 * rows])
        arrive(copies)
        image = dot3(ra_s, split(vx[k]))
        y = tri(da[...], oa[...], image)
        if k < 2:
            us.append(dot3(ra_t, split(y)) + RIDGE * vs[k])
            vs.append(us[k] * inv - SHIFTS[k] * vs[k])
            sums.append(total(vs[k + 1] * res))
    for i in range(2):
        for k in range(i, 2):
            sums.append(total(vs[i] * us[k]))
        sums.append(total(us[i] * vs[2]))
    sums.append(total(image[0:er] * y[0:er]) + RIDGE * total(vs[2] * vs[2]))

    spot = lax.broadcasted_iota(jnp.int32, (1, LANES), 1)
    mine = jnp.zeros((1, LANES), F32)
    for i, s in enumerate(sums):
        mine = jnp.where(spot == i, s, mine)
    gown[...] = mine
    gall[me] = mine

    def push(d):
        return pltpu.make_async_remote_copy(
            src_ref=gown, dst_ref=gall.at[me], send_sem=gs.at[d], recv_sem=gr.at[d],
            device_id={"wave": lax.rem(me + d, n)}, device_id_type=pl.DeviceIdType.MESH)

    @pl.loop(1, n)
    def _(d):
        push(d).start()

    us.append(dot3(ra_t, split(y)) + RIDGE * vs[2])

    @pl.loop(1, n)
    def _(d):
        push(d).wait_recv()

    whole = jnp.sum(gall[...], axis=0)
    b0, b1, b2, a00, a01, a02, a11, a12, a22 = [
        total(jnp.where(spot == i, whole, 0.0)) for i in range(9)]
    l10, l20 = a01 / a00, a02 / a00
    d1, e21 = a11 - l10 * a01, a12 - l20 * a01
    l21 = e21 / d1
    d2 = a22 - l20 * a02 - l21 * e21
    y1 = b1 - l10 * b0
    y2 = b2 - l20 * b0 - l21 * y1
    c2 = y2 / d2
    c1 = y1 / d1 - l21 * c2
    c0 = b0 / a00 - l10 * c1 - l20 * c2
    new_x = fx[rows:2 * rows, :] + (c0 * vs[0] + c1 * vs[1] + c2 * vs[2])
    new_r = res - (c0 * us[0] + c1 * us[1] + c2 * us[2])
    x_ref[...] = new_x[:, 0:fib]
    r_ref[...] = new_r[:, 0:fib]

    for copies in [flux_copies, fold_copies, row_copies] + pack_copies + v_copies:
        sent(copies)

    @pl.loop(1, n)
    def _(d):
        push(d).wait_send()


def hand_over(x_ref, r_ref, x_out, r_out):
    x_out[...] = x_ref[...]
    r_out[...] = r_ref[...]


def solution(mesh):
    n = mesh.shape["wave"]

    def local(frames, inverse_var, masked, psf_band, offsets, starts, profile, flux_start):
        expo, rows, cols = frames.shape
        fib = flux_start.shape[1]
        chunks = -(-fib // LANES)
        wide = chunks * LANES
        er, side = expo * rows, expo * REACH
        vmem, smem = pl.BlockSpec(memory_space=pltpu.VMEM), pl.BlockSpec(memory_space=pltpu.SMEM)
        far = pl.BlockSpec(memory_space=pl.ANY)
        out = jax.ShapeDtypeStruct(flux_start.shape, F32)
        dma = pltpu.SemaphoreType.DMA
        frame = (expo, rows, cols)
        found = pl.pallas_call(
            functools.partial(kernel, n, chunks=chunks),
            out_shape=(out, out),
            in_specs=[far, far, far, vmem, smem, vmem, vmem, vmem],
            out_specs=(vmem, vmem),
            scratch_shapes=[
                pltpu.VMEM(frame, F32), pltpu.VMEM(frame, F32), pltpu.VMEM(frame, jnp.int32),
                pltpu.VMEM((24, wide), F32), pltpu.VMEM((1, wide), jnp.int32),
                pltpu.VMEM((wide + PITCH, LANES), F32), pltpu.VMEM((wide + PITCH, LANES), F32),
                pltpu.VMEM((3, wide + PITCH, er), F32), pltpu.VMEM((chunks, expo, rows, 2 * LANES), F32),
                pltpu.VMEM((expo, rows, LANES), F32), pltpu.VMEM((er, wide), F32),
                pltpu.VMEM((LANES, wide), F32), pltpu.VMEM((REACH, fib), F32), pltpu.VMEM((REACH, fib), F32),
                pltpu.VMEM((chunks, expo, REACH, 2 * LANES), F32), pltpu.VMEM((chunks, expo, REACH, 2 * LANES), F32),
                pltpu.VMEM((expo, REACH, LANES), F32), pltpu.VMEM((expo, REACH, LANES), F32),
                pltpu.VMEM((2, LANES, wide), F32), pltpu.VMEM((2, REACH, wide), F32), pltpu.VMEM((2, REACH, wide), F32),
                pltpu.VMEM((3, LANES, wide), F32), pltpu.VMEM((er + 2 * side, LANES), F32),
                pltpu.VMEM((er + 2 * side, wide), F32), pltpu.VMEM((er + 2 * side, wide), F32),
                pltpu.VMEM((1, LANES), F32), pltpu.VMEM((n, 1, LANES), F32),
                dma((3, chunks)), *[dma((6 + chunks,))] * 4, dma((n,)), dma((n,)),
            ],
            compiler_params=pltpu.CompilerParams(
                collective_id=0, has_side_effects=True, vmem_limit_bytes=56 * 1024 * 1024),
        )(frames, inverse_var, masked, jnp.swapaxes(psf_band, 1, 2), offsets, starts,
          jnp.swapaxes(profile, 0, 1), flux_start)
        return pl.pallas_call(hand_over, out_shape=(out, out), in_specs=[vmem, vmem], out_specs=(vmem, vmem))(*found)

    frame = P(None, ("tile", "wave"), None)
    flat = P(("tile", "wave"), None)
    return jax.shard_map(
        local, mesh=mesh,
        in_specs=(frame, frame, frame, frame, P(("tile", "wave")), flat, P(("tile", "wave"), None, None), flat),
        out_specs=(flat, flat), check_vma=False)
```
